512 devices in a mesh: img: 32 (over y, z_hi, core), view: 16 (over x, z_lo).
Axes of the slice: x: 4, y: 4, z: 16 (z_hi: 4, z_lo: 4; z = z_hi * 4 + z_lo), core: 2. Of those that a mesh axis runs over, the one named last changes fastest.
Arguments:
- images: float32 [2, 12288, 1024], P(None, ('img', 'view')), may hold values from -30 to 30, as said below
- views: float32 [8192, 1024], P('view'), may hold values from -5 to 5, as said below
Outputs:
- new_views: float32 [8192, 1024], P('view')
The draws below stay inside these ranges and needn't reach their ends.
Inputs may be any that keep to these rules, and one draw needn't show every extreme that they name: `images`: real valued Fourier values. `views`: real valued Fourier values.
All inputs are finite; a program needn't handle non-finite values.
Results may differ from the reference program's by a relative error of at most 0.0003.
Values sent between devices are 32-bit elements; how exact they have to be, the bound alone decides.
No kernel may reach another device: no remote copies, remote signals or barrier semaphores. Data moves between devices by JAX's collectives and lax.ppermute only.
A program may use at most 64 MiB of HBM per device.

```python
import jax
import jax.numpy as jnp
from jax import lax

F = 1024
BATCH = 384
INNER = 2
ROUNDS = 1
VIEWS = 8192
IMAGES = 12288
N_IMG = 32


def common_views(key):
    base_views = jnp.clip(jax.random.normal(jax.random.fold_in(key, 1), (VIEWS, F), jnp.float32), -4.5, 4.5)
    return base_views


def draw_views(key, part):
    return common_views(jax.random.fold_in(key, 11))


def draw_images(key, part):
    pictures = jnp.clip(jax.random.normal(jax.random.fold_in(key, 21), (INNER * IMAGES, F), jnp.float32), -5.0, 5.0)
    return pictures.reshape(INNER, IMAGES, F)


def setup_inputs(seed: int = 0) -> dict:
    keys = jax.random.split(jax.random.key(seed), 3)
    return {
        "images": draw_images(jax.random.fold_in(keys[2], 71), 0),
        "views": draw_views(jax.random.fold_in(keys[2], 71), 0),
    }


def reference(images, views):
    beta = 1.6 / jnp.sqrt(jnp.float32(F))
    current = views
    for em_round in range(ROUNDS):
        half_norm = 0.5 * lax.optimization_barrier(jnp.sum(current * current, axis=1))

        def group_step(carry, group_id):
            res_acc, mass_acc = carry
            start = (group_id * BATCH).astype(jnp.int32)
            group_rows = lax.dynamic_slice_in_dim(images, start, BATCH, 1).reshape(INNER * BATCH, F)
            scores = beta * (jnp.dot(group_rows, current.T, precision=lax.Precision.HIGHEST) - half_norm)
            peak = lax.optimization_barrier(jnp.max(scores, axis=1, keepdims=True))
            expo = jnp.exp(scores - peak)
            post = expo / lax.optimization_barrier(jnp.sum(expo, axis=1, keepdims=True))
            numerator = jnp.dot(post.T, group_rows, precision=lax.Precision.HIGHEST)
            weight_mass = lax.optimization_barrier(jnp.sum(post, axis=0))
            residual_sum = numerator - weight_mass[:, None] * current
            return ((res_acc + residual_sum, mass_acc + weight_mass), None)
        start_carry = (jnp.zeros((VIEWS, F), jnp.float32), jnp.zeros((VIEWS,), jnp.float32))
        (res_total, mass_total), unused = lax.scan(group_step, start_carry, jnp.arange(N_IMG, dtype=jnp.int32))
        current = current + res_total / (mass_total[:, None] + 1.0)
    return current
```

```python
import math

import jax
import jax.numpy as jnp
from jax import lax
from jax.sharding import Mesh, PartitionSpec as P

F = 1024
LANES = 128
AXES = ("y", "zh", "c", "x", "zl")
VIEW = ("x", "zl")
BETA = 1.6 / math.sqrt(F)


def spread(block, axis, n):
    return lax.all_to_all(jnp.broadcast_to(block[None], (n,) + block.shape), axis, 0, 0)


def gather_images(images):
    own = images.reshape(-1, F)
    line = lax.all_gather(own, "zl", axis=0, tiled=True)
    return spread(line, "x", 4).reshape(-1, F)


def tiles(rows):
    p = rows.shape[0]
    return rows.reshape(p, 2, 8, 8, LANES).transpose(0, 1, 3, 2, 4).reshape(p, 16, 8, LANES)


def untile(blocks):
    p = blocks.shape[0]
    return blocks.reshape(p, 2, 8, 8, LANES).transpose(0, 1, 3, 2, 4).reshape(p, 16, F)


def on_device(images, views):
    n_views = views.shape[0]
    gathered = gather_images(images)
    n = gathered.shape[0]
    half_norm = 0.5 * jnp.sum(views * views, axis=1, keepdims=True)
    scores = BETA * (
        lax.dot_general(views, gathered, (((1,), (1,)), ((), ())), precision=lax.Precision.HIGH) - half_norm
    )
    local_max = jnp.max(scores, axis=0)
    expo = jnp.exp(scores - local_max)
    local_sum = jnp.sum(expo, axis=0)
    stats = jnp.concatenate([local_max.reshape(-1, LANES), local_sum.reshape(-1, LANES)])
    every = spread(stats, VIEW, 16)
    maxes = every[:, : n // LANES].reshape(16, n)
    sums = every[:, n // LANES :].reshape(16, n)
    peak = jnp.max(maxes, axis=0)
    total = jnp.sum(sums * jnp.exp(maxes - peak), axis=0)
    weights = expo * (jnp.exp(local_max - peak) / total)
    numerator = jnp.dot(weights, gathered, precision=lax.Precision.HIGH)
    mass = jnp.sum(weights, axis=1)
    pieces = n_views // 16
    mass_tile = jnp.broadcast_to(
        mass.reshape(pieces, 2, 8).transpose(0, 2, 1)[:, :, :, None], (pieces, 8, 2, 64)
    ).reshape(pieces, 1, 8, LANES)
    packed = jnp.concatenate([tiles(numerator.reshape(pieces, 16, F)), mass_tile], axis=1)
    packed = packed.reshape(2, pieces // 2, 17, 8, LANES)
    core = lax.axis_index("c")
    mine = lax.dynamic_index_in_dim(packed, core, 0, keepdims=False)
    theirs = lax.dynamic_index_in_dim(packed, 1 - core, 0, keepdims=False)
    mine = mine + lax.ppermute(theirs, "c", [(0, 1), (1, 0)])
    mine = lax.all_to_all(mine.reshape(4, 4, 17, 8, LANES), "y", 0, 0).sum(axis=0)
    mine = lax.all_to_all(mine, "zh", 0, 0).sum(axis=0)
    place = (core * 4 + lax.axis_index("y")) * 4 + lax.axis_index("zh")
    current = tiles(lax.dynamic_slice_in_dim(views, place * 16, 16, 0)[None])[0]
    num, mass = mine[:16].reshape(2, 8, 8, LANES), mine[16]
    mass = jnp.stack([mass[:, :1], mass[:, 64:65]])[:, None]
    new = (current.reshape(2, 8, 8, LANES) + num) / (mass + 1.0)
    new = new.reshape(16, 8, LANES)
    new = lax.all_gather(new, "zh", axis=0)
    new = spread(new, "y", 4)
    other = lax.ppermute(new, "c", [(0, 1), (1, 0)])
    both = jnp.where(core == 0, jnp.stack([new, other]), jnp.stack([other, new]))
    return untile(both.reshape(pieces, 16, 8, LANES)).reshape(n_views, F)


def solution(mesh):
    inner = Mesh(mesh.devices.reshape(4, 4, 2, 4, 4), AXES)
    placed = (P(None, AXES, None), P(VIEW, None))
    return jax.shard_map(
        on_device, mesh=inner, in_specs=placed, out_specs=P(VIEW, None), check_vma=False
    )
```

```python
import math

import jax
import jax.numpy as jnp
from jax import lax
from jax.experimental import pallas as pl
from jax.experimental.pallas import tpu as pltpu
from jax.sharding import Mesh, PartitionSpec as P

F = 1024
LANES = 128
BLOCK = 192
HALF = 256
ROWS = 64
CUT = 32
AXES = ("y", "zh", "c", "x", "zl")
VIEW = ("x", "zl")
BETA = 1.6 / math.sqrt(F)
SWAP = [(0, 1), (1, 0)]
UP = [(i, (i + 1) % 4) for i in range(4)]
DOWN = [(i, (i - 1) % 4) for i in range(4)]
EVEN = [(0, 1), (1, 0), (2, 3), (3, 2)]
ODD = [(1, 2), (2, 1), (3, 0), (0, 3)]
VMEM = pl.BlockSpec(memory_space=pltpu.VMEM)
SMEM = pl.BlockSpec(memory_space=pltpu.SMEM)
BF16, F32 = jnp.bfloat16, jnp.float32


def shape(*dims, dtype=F32):
    return jax.ShapeDtypeStruct(dims, dtype)


def split(x):
    high = x.astype(BF16)
    return high, (x - high.astype(F32)).astype(BF16)


def product(a, b, dims):
    def dot(p, q):
        return lax.dot_general(p, q, (dims, ((), ())), preferred_element_type=F32)

    return dot(a[0], b[0]) + (dot(a[0], b[1]) + dot(a[1], b[0]))


def call(body, out, n_in, flops, name, smem=0):
    return pl.pallas_call(
        body,
        out_shape=out,
        in_specs=[SMEM] * smem + [VMEM] * n_in,
        out_specs=jax.tree.map(lambda _: VMEM, out),
        cost_estimate=pl.CostEstimate(flops=flops, bytes_accessed=4 << 20, transcendentals=0),
        compiler_params=pltpu.CompilerParams(vmem_limit_bytes=16 << 20),
        name=name,
    )


def prepare_body(views, high, low, norm):
    v = views[...]
    high[...], low[...] = split(v)
    norm[...] = jnp.broadcast_to(0.5 * jnp.sum(v * v, axis=1, keepdims=True), norm.shape)


def score(views, parts, e, stats, high, low):
    x = [r[...] for r in parts]
    x = x[0] if len(x) == 1 else jnp.concatenate(x, axis=0)
    pair = split(x)
    high[...], low[...] = pair
    dots = product((views[0][...], views[1][...]), pair, ((1,), (1,)))
    s = BETA * (dots - views[2][:, :1])
    peak = jnp.max(s, axis=0, keepdims=True)
    expo = jnp.exp(s - peak)
    e[...] = expo
    stats[...] = jnp.concatenate([peak, jnp.sum(expo, axis=0, keepdims=True)], axis=0)


def block_out(v):
    return [shape(v, BLOCK), shape(2, BLOCK), shape(BLOCK, F, dtype=BF16), shape(BLOCK, F, dtype=BF16)]


def near_body(*refs):
    views, n = refs[:3], (len(refs) - 3) // 5
    parts, outs = refs[3 : 3 + n], refs[3 + n :]
    for k in range(n):
        score(views, parts[k : k + 1], *outs[4 * k : 4 * k + 4])


def near(prepared, lines, name):
    v = prepared[0].shape[0]
    out = block_out(v) * len(lines)
    got = call(near_body, out, 3 + len(lines), 6 * len(lines) * BLOCK * v * F, name)(*prepared, *lines)
    return [got[k : k + 4] for k in range(0, len(got), 4)]


def far_body(where, vh, vl, vn, a, b, s0, s1, s3, e, stats, high, low, every):
    score((vh, vl, vn), (a, b), e, stats, high, low)
    for o, s in enumerate((s0, s1, stats, s3)):
        line = lax.rem(where[0] + o, 4)
        for k in range(16):
            every[k, line] = s[...]


def far(where, prepared, a, b, stats):
    v = prepared[0].shape[0]
    out = block_out(v) + [shape(16, 4, 2, BLOCK)]
    got = call(far_body, out, 8, 6 * BLOCK * v * F, "scores_far", smem=1)(where, *prepared, a, b, *stats)
    return got[:4], got[4]


def numerator_body(own, where, every, *refs):
    out = refs[-1]
    core = where[1] if own else 1 - where[1]
    start = pl.multiple_of(core * HALF, HALF)
    acc = jnp.zeros((HALF, F), F32)
    mass = jnp.zeros((HALF, 1), F32)
    for o in range(4):
        e, local, high, low = refs[4 * o : 4 * o + 4]
        stats = every[:, lax.rem(where[0] + o, 4)]
        maxes, sums = stats[:, 0], stats[:, 1]
        peak = jnp.max(maxes, axis=0, keepdims=True)
        total = jnp.sum(sums * jnp.exp(maxes - peak), axis=0, keepdims=True)
        w = e[pl.ds(start, HALF), :] * (jnp.exp(local[0:1] - peak) / total)
        mass = mass + jnp.sum(w, axis=1, keepdims=True)
        acc = acc + product(split(w), (high[...], low[...]), ((1,), (0,)))
    lane = lax.broadcasted_iota(jnp.int32, (8, LANES), 1) // 16
    for y in range(4):
        held = jnp.zeros((8, LANES), F32)
        for r in range(8):
            row = y * ROWS + r * 8
            for t in range(8):
                out[y, r * 8 + t] = acc[row : row + 8, t * LANES : (t + 1) * LANES]
            held = jnp.where(lane == r, mass[row : row + 8], held)
        out[y, ROWS] = held


def numerator(own, where, every, blocks, name):
    flat = [a for block in blocks for a in block]
    body = lambda *refs: numerator_body(own, *refs)
    out = shape(4, ROWS + 1, 8, LANES)
    return call(body, out, 1 + len(flat), 24 * HALF * BLOCK * F, name, smem=1)(where, every, *flat)


def gather_body(parts, even, odd):
    total = (parts[0] + parts[1]) + (parts[2] + parts[3])
    even[...], odd[...] = total[:CUT], total[CUT:]


def gather(parts):
    out = [shape(CUT, 8, LANES), shape(ROWS + 1 - CUT, 8, LANES)]
    return call(gather_body, out, 1, 4 * ROWS * F, "sum_y")(parts)


def update_body(current, even, even_got, odd, odd_got, out):
    mass = odd[ROWS - CUT] + odd_got[ROWS - CUT] + 1.0
    for r in range(8):
        scale = mass[:, 16 * r : 16 * r + 1]
        for t in range(8):
            k = r * 8 + t
            here = current[r * 8 : r * 8 + 8, t * LANES : (t + 1) * LANES]
            got = even[k] + even_got[k] if k < CUT else odd[k - CUT] + odd_got[k - CUT]
            new = (here + got) / scale
            for y in range(4):
                out[y, k] = new


def update(*args):
    return call(update_body, shape(4, ROWS, 8, LANES), 5, 4 * ROWS * F, "update")(*args)


def on_device(images, views):
    core, y, x = lax.axis_index("c"), lax.axis_index("y"), lax.axis_index("x")
    n_views = views.shape[0]
    where = jnp.stack([x, core]).astype(jnp.int32)
    lower = core == 0
    current = lax.dynamic_slice_in_dim(views, core * HALF + y * ROWS, ROWS, 0)
    images, views, where, lower, current = lax.optimization_barrier((images, views, where, lower, current))
    own = lax.all_gather(images.reshape(-1, F), "zl", axis=0, tiled=True)
    up = lax.ppermute(own, "x", UP)
    down = lax.ppermute(own, "x", DOWN)
    half = BLOCK // 2
    far_a = lax.ppermute(up[:half], "x", UP)
    far_b = lax.ppermute(down[half:], "x", DOWN)
    prepared = call(
        prepare_body,
        [shape(n_views, F, dtype=BF16), shape(n_views, F, dtype=BF16), shape(n_views, LANES)],
        1, 4 * n_views * F, "prepare",
    )(views)
    (b_own,) = near(prepared, (own,), "scores_own")
    b_up, b_down = near(prepared, (up, down), "scores_near")
    b_far, every = far(where, prepared, far_a, far_b, (b_own[1], b_down[1], b_up[1]))
    every = lax.all_to_all(every, VIEW, 0, 0)
    blocks = (b_own, b_down, b_far, b_up)
    theirs = lax.ppermute(numerator(False, where, every, blocks, "numerator_theirs"), "c", SWAP)
    mine = numerator(True, where, every, blocks, "numerator_mine") + theirs
    even, odd = gather(lax.all_to_all(mine, "y", 0, 0))
    even, odd = even + lax.ppermute(even, "zh", EVEN), odd + lax.ppermute(odd, "zh", ODD)
    new = update(current, even, lax.ppermute(even, "zh", ODD), odd, lax.ppermute(odd, "zh", EVEN))
    new = lax.all_to_all(new, "y", 0, 0)
    other = lax.ppermute(new, "c", SWAP)
    both = jnp.where(lower, jnp.stack([new, other]), jnp.stack([other, new]))
    return both.reshape(n_views // 8, 8, 8, LANES).transpose(0, 2, 1, 3).reshape(n_views, F)


def solution(mesh):
    inner = Mesh(mesh.devices.reshape(4, 4, 2, 4, 4), AXES)
    placed = (P(None, AXES, None), P(VIEW, None))
    return jax.shard_map(
        on_device, mesh=inner, in_specs=placed, out_specs=P(VIEW, None), check_vma=False
    )
```

```python
import math

import jax
import jax.numpy as jnp
from jax import lax
from jax.experimental import pallas as pl
from jax.experimental.pallas import tpu as pltpu
from jax.sharding import Mesh, PartitionSpec as P

F = 1024
LANES = 128
BLOCK = 192
HALF = 256
ROWS = 64
AXES = ("y", "zh", "c", "x", "zl")
VIEW = ("x", "zl")
BETA = 1.6 / math.sqrt(F)
SWAP = [(0, 1), (1, 0)]
UP = [(i, (i + 1) % 4) for i in range(4)]
DOWN = [(i, (i - 1) % 4) for i in range(4)]
EVEN, ODD = [(0, 1), (2, 3)], [(1, 2), (3, 0)]
CROSS = [[2 * a, 2 * b] for a, b in EVEN] + [[2 * a + 1, 2 * b + 1] for a, b in ODD]
UNCROSS = [[2 * a, 2 * b] for a, b in ODD] + [[2 * a + 1, 2 * b + 1] for a, b in EVEN]
VMEM = pl.BlockSpec(memory_space=pltpu.VMEM)
SMEM = pl.BlockSpec(memory_space=pltpu.SMEM)
BF16, F32 = jnp.bfloat16, jnp.float32


def shape(*dims, dtype=F32):
    return jax.ShapeDtypeStruct(dims, dtype)


def split(x):
    high = x.astype(BF16)
    return high, (x - high.astype(F32)).astype(BF16)


def product(a, b, dims):
    def dot(p, q):
        return lax.dot_general(p, q, (dims, ((), ())), preferred_element_type=F32)

    return dot(a[0], b[0]) + (dot(a[0], b[1]) + dot(a[1], b[0]))


def call(body, out, n_in, flops, name, smem=0):
    return pl.pallas_call(
        body,
        out_shape=out,
        in_specs=[SMEM] * smem + [VMEM] * n_in,
        out_specs=jax.tree.map(lambda _: VMEM, out),
        cost_estimate=pl.CostEstimate(flops=flops, bytes_accessed=4 << 20, transcendentals=0),
        compiler_params=pltpu.CompilerParams(vmem_limit_bytes=16 << 20),
        name=name,
    )


def prepare_body(views, high, low, norm):
    v = views[...]
    high[...], low[...] = split(v)
    norm[...] = jnp.broadcast_to(0.5 * jnp.sum(v * v, axis=1, keepdims=True), norm.shape)


def score(views, parts, e, stats, high, low):
    x = [r[...] for r in parts]
    x = x[0] if len(x) == 1 else jnp.concatenate(x, axis=0)
    pair = split(x)
    high[...], low[...] = pair
    dots = product((views[0][...], views[1][...]), pair, ((1,), (1,)))
    s = BETA * (dots - views[2][:, :1])
    peak = jnp.max(s, axis=0, keepdims=True)
    expo = jnp.exp(s - peak)
    e[...] = expo
    stats[...] = jnp.concatenate([peak, jnp.sum(expo, axis=0, keepdims=True)], axis=0)


def block_out(v):
    return [shape(v, BLOCK), shape(2, BLOCK), shape(BLOCK, F, dtype=BF16), shape(BLOCK, F, dtype=BF16)]


def near_body(*refs):
    views, n = refs[:3], (len(refs) - 3) // 5
    parts, outs = refs[3 : 3 + n], refs[3 + n :]
    for k in range(n):
        score(views, parts[k : k + 1], *outs[4 * k : 4 * k + 4])


def near(prepared, lines, name):
    v = prepared[0].shape[0]
    out = block_out(v) * len(lines)
    got = call(near_body, out, 3 + len(lines), 6 * len(lines) * BLOCK * v * F, name)(*prepared, *lines)
    return [got[k : k + 4] for k in range(0, len(got), 4)]


def far_body(where, vh, vl, vn, a, b, s0, s1, s3, e, stats, high, low, every):
    score((vh, vl, vn), (a, b), e, stats, high, low)
    for o, s in enumerate((s0, s1, stats, s3)):
        line = lax.rem(where[0] + o, 4)
        for k in range(16):
            every[k, line] = s[...]


def far(where, prepared, a, b, stats):
    v = prepared[0].shape[0]
    out = block_out(v) + [shape(16, 4, 2, BLOCK)]
    got = call(far_body, out, 8, 6 * BLOCK * v * F, "scores_far", smem=1)(where, *prepared, a, b, *stats)
    return got[:4], got[4]


def numerator_body(own, where, every, *refs):
    out = refs[-1]
    core = where[1] if own else 1 - where[1]
    start = pl.multiple_of(core * HALF, HALF)
    acc = jnp.zeros((HALF, F), F32)
    mass = jnp.zeros((HALF, 1), F32)
    for o in range(4):
        e, local, high, low = refs[4 * o : 4 * o + 4]
        stats = every[:, lax.rem(where[0] + o, 4)]
        maxes, sums = stats[:, 0], stats[:, 1]
        peak = jnp.max(maxes, axis=0, keepdims=True)
        total = jnp.sum(sums * jnp.exp(maxes - peak), axis=0, keepdims=True)
        w = e[pl.ds(start, HALF), :] * (jnp.exp(local[0:1] - peak) / total)
        mass = mass + jnp.sum(w, axis=1, keepdims=True)
        acc = acc + product(split(w), (high[...], low[...]), ((1,), (0,)))
    lane = lax.broadcasted_iota(jnp.int32, (8, LANES), 1) // 16
    for y in range(4):
        held = jnp.zeros((8, LANES), F32)
        for r in range(8):
            row = y * ROWS + r * 8
            for t in range(8):
                out[y, r * 8 + t] = acc[row : row + 8, t * LANES : (t + 1) * LANES]
            held = jnp.where(lane == r, mass[row : row + 8], held)
        out[y, ROWS] = held


def numerator(own, where, every, blocks, name):
    flat = [a for block in blocks for a in block]
    body = lambda *refs: numerator_body(own, *refs)
    out = shape(4, ROWS + 1, 8, LANES)
    return call(body, out, 1 + len(flat), 24 * HALF * BLOCK * F, name, smem=1)(where, every, *flat)


def gather_body(parts, out):
    out[...] = (parts[0] + parts[1]) + (parts[2] + parts[3])


def gather(parts):
    return call(gather_body, shape(ROWS + 1, 8, LANES), 1, 4 * ROWS * F, "sum_y")(parts)


def update_body(where, views, sums, out):
    start = pl.multiple_of(where[2], ROWS)
    mass = sums[0, ROWS] + sums[1, ROWS] + 1.0
    for r in range(8):
        scale = mass[:, 16 * r : 16 * r + 1]
        for t in range(8):
            k = r * 8 + t
            here = views[pl.ds(start + r * 8, 8), t * LANES : (t + 1) * LANES]
            new = (here + (sums[0, k] + sums[1, k])) / scale
            for y in range(4):
                out[y, k] = new


def update(*args):
    return call(update_body, shape(4, ROWS, 8, LANES), 2, 4 * ROWS * F, "update", smem=1)(*args)


def on_device(images, views):
    core, y, x = lax.axis_index("c"), lax.axis_index("y"), lax.axis_index("x")
    n_views = views.shape[0]
    images, core, x, row, lower = lax.optimization_barrier((images, core, x, core * HALF + y * ROWS, core == 0))
    where = jnp.stack([x, core, row]).astype(jnp.int32)
    own = lax.all_gather(images.reshape(-1, F), "zl", axis=0, tiled=True)
    up = lax.ppermute(own, "x", UP)
    down = lax.ppermute(own, "x", DOWN)
    half = BLOCK // 2
    far_a = lax.ppermute(up[:half], "x", UP)
    far_b = lax.ppermute(down[half:], "x", DOWN)
    prepared = call(
        prepare_body,
        [shape(n_views, F, dtype=BF16), shape(n_views, F, dtype=BF16), shape(n_views, LANES)],
        1, 4 * n_views * F, "prepare",
    )(views)
    (b_own,) = near(prepared, (own,), "scores_own")
    b_up, b_down = near(prepared, (up, down), "scores_near")
    b_far, every = far(where, prepared, far_a, far_b, (b_own[1], b_down[1], b_up[1]))
    every = lax.all_to_all(every, VIEW, 0, 0)
    blocks = (b_own, b_down, b_far, b_up)
    theirs = lax.ppermute(numerator(False, where, every, blocks, "numerator_theirs"), "c", SWAP)
    mine = numerator(True, where, every, blocks, "numerator_mine") + theirs
    sums = gather(lax.all_to_all(mine, "y", 0, 0))
    pair = lax.all_gather(sums, ("zh", "c"), axis=0, axis_index_groups=CROSS)
    sums = lax.all_gather(pair[0] + pair[1], ("zh", "c"), axis=0, axis_index_groups=UNCROSS)
    new = update(where, views, sums)
    new = lax.all_to_all(new, "y", 0, 0)
    other = lax.ppermute(new, "c", SWAP)
    both = jnp.where(lower, jnp.stack([new, other]), jnp.stack([other, new]))
    return both.reshape(n_views // 8, 8, 8, LANES).transpose(0, 2, 1, 3).reshape(n_views, F)


def solution(mesh):
    inner = Mesh(mesh.devices.reshape(4, 4, 2, 4, 4), AXES)
    placed = (P(None, AXES, None), P(VIEW, None))
    return jax.shard_map(
        on_device, mesh=inner, in_specs=placed, out_specs=P(VIEW, None), check_vma=False
    )
```

```python
import math

import jax
import jax.numpy as jnp
from jax import lax
from jax.experimental import pallas as pl
from jax.experimental.pallas import tpu as pltpu
from jax.sharding import Mesh, PartitionSpec as P

F = 1024
LANES = 128
BLOCK = 192
HALF = 256
ROWS = 64
AXES = ("y", "zh", "c", "x", "zl")
VIEW = ("x", "zl")
BETA = 1.6 / math.sqrt(F)
SWAP = [(0, 1), (1, 0)]
UP = [(i, (i + 1) % 4) for i in range(4)]
DOWN = [(i, (i - 1) % 4) for i in range(4)]
ACROSS = [(i, (i + 2) % 4) for i in range(4)]
EVEN, ODD = [(0, 1), (2, 3)], [(1, 2), (3, 0)]
CROSS = [[2 * a, 2 * b] for a, b in EVEN] + [[2 * a + 1, 2 * b + 1] for a, b in ODD]
UNCROSS = [[2 * a, 2 * b] for a, b in ODD] + [[2 * a + 1, 2 * b + 1] for a, b in EVEN]
VMEM = pl.BlockSpec(memory_space=pltpu.VMEM)
SMEM = pl.BlockSpec(memory_space=pltpu.SMEM)
BF16, F32 = jnp.bfloat16, jnp.float32


def shape(*dims, dtype=F32):
    return jax.ShapeDtypeStruct(dims, dtype)


def split(x):
    high = x.astype(BF16)
    return high, (x - high.astype(F32)).astype(BF16)


def product(a, b, dims):
    def dot(p, q):
        return lax.dot_general(p, q, (dims, ((), ())), preferred_element_type=F32)

    return dot(a[0], b[0]) + (dot(a[0], b[1]) + dot(a[1], b[0]))


def call(body, out, n_in, flops, smem=0):
    return pl.pallas_call(
        body,
        out_shape=out,
        in_specs=[SMEM] * smem + [VMEM] * n_in,
        out_specs=jax.tree.map(lambda _: VMEM, out),
        cost_estimate=pl.CostEstimate(flops=flops, bytes_accessed=4 << 20, transcendentals=0),
        compiler_params=pltpu.CompilerParams(vmem_limit_bytes=16 << 20),
    )


def prepare_body(views, high, low, norm):
    v = views[...]
    high[...], low[...] = split(v)
    norm[...] = jnp.broadcast_to(0.5 * jnp.sum(v * v, axis=1, keepdims=True), norm.shape)


def score(views, images, e, stats, high, low):
    pair = split(images[...])
    high[...], low[...] = pair
    dots = product((views[0][...], views[1][...]), pair, ((1,), (1,)))
    s = BETA * (dots - views[2][:, :1])
    peak = jnp.max(s, axis=0, keepdims=True)
    expo = jnp.exp(s - peak)
    e[...] = expo
    stats[...] = jnp.concatenate([peak, jnp.sum(expo, axis=0, keepdims=True)], axis=0)


def block_out(v):
    return [shape(v, BLOCK), shape(2, BLOCK), shape(BLOCK, F, dtype=BF16), shape(BLOCK, F, dtype=BF16)]


def some_body(*refs):
    views, n = refs[:3], (len(refs) - 3) // 5
    blocks, outs = refs[3 : 3 + n], refs[3 + n :]
    for k in range(n):
        score(views, blocks[k], *outs[4 * k : 4 * k + 4])


def some(prepared, blocks):
    v, n = prepared[0].shape[0], len(blocks)
    got = call(some_body, block_out(v) * n, 3 + n, 6 * n * BLOCK * v * F)(*prepared, *blocks)
    return [got[k : k + 4] for k in range(0, len(got), 4)]


def rest_body(where, *refs):
    views, blocks, known, outs, every = refs[:3], refs[3:5], refs[5:7], refs[7:15], refs[15]
    for k in range(2):
        score(views, blocks[k], *outs[4 * k : 4 * k + 4])
    for o, s in enumerate((known[0], outs[1], known[1], outs[5])):
        line = lax.rem(where[0] + o, 4)
        for k in range(16):
            every[k, line] = s[...]


def rest(where, prepared, blocks, stats):
    v = prepared[0].shape[0]
    out = block_out(v) * 2 + [shape(16, 4, 2, BLOCK)]
    got = call(rest_body, out, 7, 12 * BLOCK * v * F, smem=1)(where, *prepared, *blocks, *stats)
    return got[:4], got[4:8], got[8]


def numerator_body(own, where, every, *refs):
    out = refs[-1]
    core = where[1] if own else 1 - where[1]
    start = pl.multiple_of(core * HALF, HALF)
    acc = jnp.zeros((HALF, F), F32)
    mass = jnp.zeros((HALF, 1), F32)
    for o in range(4):
        e, local, high, low = refs[4 * o : 4 * o + 4]
        stats = every[:, lax.rem(where[0] + o, 4)]
        maxes, sums = stats[:, 0], stats[:, 1]
        peak = jnp.max(maxes, axis=0, keepdims=True)
        total = jnp.sum(sums * jnp.exp(maxes - peak), axis=0, keepdims=True)
        w = e[pl.ds(start, HALF), :] * (jnp.exp(local[0:1] - peak) / total)
        mass = mass + jnp.sum(w, axis=1, keepdims=True)
        acc = acc + product(split(w), (high[...], low[...]), ((1,), (0,)))
    lane = lax.broadcasted_iota(jnp.int32, (8, LANES), 1) // 16
    for y in range(4):
        held = jnp.zeros((8, LANES), F32)
        for r in range(8):
            row = y * ROWS + r * 8
            for t in range(8):
                out[y, r * 8 + t] = acc[row : row + 8, t * LANES : (t + 1) * LANES]
            held = jnp.where(lane == r, mass[row : row + 8], held)
        out[y, ROWS] = held


def numerator(own, where, every, blocks):
    flat = [a for block in blocks for a in block]
    body = lambda *refs: numerator_body(own, *refs)
    out = shape(4, ROWS + 1, 8, LANES)
    return call(body, out, 1 + len(flat), 24 * HALF * BLOCK * F, smem=1)(where, every, *flat)


def gather_body(parts, out):
    out[...] = (parts[0] + parts[1]) + (parts[2] + parts[3])


def gather(parts):
    return call(gather_body, shape(ROWS + 1, 8, LANES), 1, 4 * ROWS * F)(parts)


def update_body(where, views, sums, out):
    start = pl.multiple_of(where[2], ROWS)
    mass = sums[0, ROWS] + sums[1, ROWS] + 1.0
    for r in range(8):
        scale = mass[:, 16 * r : 16 * r + 1]
        for t in range(8):
            k = r * 8 + t
            here = views[pl.ds(start + r * 8, 8), t * LANES : (t + 1) * LANES]
            new = (here + (sums[0, k] + sums[1, k])) / scale
            for y in range(4):
                out[y, k] = new


def update(*args):
    return call(update_body, shape(4, ROWS, 8, LANES), 2, 4 * ROWS * F, smem=1)(*args)


def em_round(images, views):
    core, y, x = lax.axis_index("c"), lax.axis_index("y"), lax.axis_index("x")
    n_views = views.shape[0]
    images, core, x, row, lower = lax.optimization_barrier((images, core, x, core * HALF + y * ROWS, core == 0))
    where = jnp.stack([x, core, row]).astype(jnp.int32)
    rows = images.reshape(-1, F)
    across = lax.ppermute(rows, "x", ACROSS)
    own = lax.all_gather(rows, "zl", axis=0, tiled=True)
    up = lax.ppermute(own, "x", UP)
    down = lax.ppermute(own, "x", DOWN)
    across, own = lax.optimization_barrier((across, own))
    far = lax.all_gather(across, "zl", axis=0, tiled=True)
    prepared = call(
        prepare_body,
        [shape(n_views, F, dtype=BF16), shape(n_views, F, dtype=BF16), shape(n_views, LANES)],
        1, 4 * n_views * F,
    )(views)
    b_own, b_far = some(prepared, (own, far))
    b_down, b_up, every = rest(where, prepared, (down, up), (b_own[1], b_far[1]))
    every = lax.all_to_all(every, VIEW, 0, 0)
    blocks = (b_own, b_down, b_far, b_up)
    theirs = lax.ppermute(numerator(False, where, every, blocks), "c", SWAP)
    mine = numerator(True, where, every, blocks) + theirs
    sums = gather(lax.all_to_all(mine, "y", 0, 0))
    pair = lax.all_gather(sums, ("zh", "c"), axis=0, axis_index_groups=CROSS)
    sums = lax.all_gather(pair[0] + pair[1], ("zh", "c"), axis=0, axis_index_groups=UNCROSS)
    new = update(where, views, sums)
    new = lax.all_to_all(new, "y", 0, 0)
    other = lax.ppermute(new, "c", SWAP)
    both = jnp.where(lower, jnp.stack([new, other]), jnp.stack([other, new]))
    return both.reshape(n_views // 8, 8, 8, LANES).transpose(0, 2, 1, 3).reshape(n_views, F)


def solution(mesh):
    inner = Mesh(mesh.devices.reshape(4, 4, 2, 4, 4), AXES)
    placed = (P(None, AXES, None), P(VIEW, None))
    return jax.shard_map(em_round, mesh=inner, in_specs=placed, out_specs=P(VIEW, None), check_vma=False)
```

```python
import math

import jax
import jax.numpy as jnp
from jax import lax
from jax.experimental import pallas as pl
from jax.experimental.pallas import tpu as pltpu
from jax.sharding import Mesh, PartitionSpec as P

F = 1024
LANES = 128
BLOCK = 192
HALF = 256
ROWS = 64
AXES = ("y", "zh", "c", "x", "zl")
VIEW = ("x", "zl")
BETA = 1.6 / math.sqrt(F)
SWAP = [(0, 1), (1, 0)]
UP = [(i, (i + 1) % 4) for i in range(4)]
DOWN = [(i, (i - 1) % 4) for i in range(4)]
ACROSS = [(i, (i + 2) % 4) for i in range(4)]
EVEN, ODD = [(0, 1), (2, 3)], [(1, 2), (3, 0)]
CROSS = [[2 * a, 2 * b] for a, b in EVEN] + [[2 * a + 1, 2 * b + 1] for a, b in ODD]
UNCROSS = [[2 * a, 2 * b] for a, b in ODD] + [[2 * a + 1, 2 * b + 1] for a, b in EVEN]
VMEM = pl.BlockSpec(memory_space=pltpu.VMEM)
SMEM = pl.BlockSpec(memory_space=pltpu.SMEM)
BF16, F32 = jnp.bfloat16, jnp.float32


def shape(*dims, dtype=F32):
    return jax.ShapeDtypeStruct(dims, dtype)


def split(x):
    high = x.astype(BF16)
    return high, (x - high.astype(F32)).astype(BF16)


def product(a, b, dims):
    def dot(p, q):
        return lax.dot_general(p, q, (dims, ((), ())), preferred_element_type=F32)

    return dot(a[0], b[0]) + (dot(a[0], b[1]) + dot(a[1], b[0]))


def call(body, out, n_in, flops, smem=0):
    return pl.pallas_call(
        body,
        out_shape=out,
        in_specs=[SMEM] * smem + [VMEM] * n_in,
        out_specs=jax.tree.map(lambda _: VMEM, out),
        cost_estimate=pl.CostEstimate(flops=flops, bytes_accessed=4 << 20, transcendentals=0),
        compiler_params=pltpu.CompilerParams(vmem_limit_bytes=16 << 20),
    )


def half_norm(high, low):
    v = high[...].astype(F32) + low[...].astype(F32)
    return 0.5 * jnp.sum(v * v, axis=1, keepdims=True)


def score(views, norm, images, e, stats, high, low):
    pair = split(images[...])
    high[...], low[...] = pair
    dots = product((views[0][...], views[1][...]), pair, ((1,), (1,)))
    s = BETA * (dots - norm)
    peak = jnp.max(s, axis=0, keepdims=True)
    expo = jnp.exp(s - peak)
    e[...] = expo
    stats[...] = jnp.concatenate([peak, jnp.sum(expo, axis=0, keepdims=True)], axis=0)


def block_out(v):
    return [shape(v, BLOCK), shape(2, BLOCK), shape(BLOCK, F, dtype=BF16), shape(BLOCK, F, dtype=BF16)]


def some_body(*refs):
    views, n = refs[:2], (len(refs) - 2) // 5
    blocks, outs = refs[2 : 2 + n], refs[2 + n :]
    norm = half_norm(*views)
    for k in range(n):
        score(views, norm, blocks[k], *outs[4 * k : 4 * k + 4])


def some(prepared, blocks):
    v, n = prepared[0].shape[0], len(blocks)
    got = call(some_body, block_out(v) * n, 2 + n, 6 * n * BLOCK * v * F)(*prepared, *blocks)
    return [got[k : k + 4] for k in range(0, len(got), 4)]


def rest_body(where, *refs):
    views, blocks, known, outs, every = refs[:2], refs[2:4], refs[4:6], refs[6:14], refs[14]
    norm = half_norm(*views)
    for k in range(2):
        score(views, norm, blocks[k], *outs[4 * k : 4 * k + 4])
    for o, s in enumerate((known[0], outs[1], known[1], outs[5])):
        line = lax.rem(where[0] + o, 4)
        for k in range(16):
            every[k, line] = s[...]


def rest(where, prepared, blocks, stats):
    v = prepared[0].shape[0]
    out = block_out(v) * 2 + [shape(16, 4, 2, BLOCK)]
    got = call(rest_body, out, 6, 12 * BLOCK * v * F, smem=1)(where, *prepared, *blocks, *stats)
    return got[:4], got[4:8], got[8]


def numerator_body(own, where, every, *refs):
    out = refs[-1]
    core = where[1] if own else 1 - where[1]
    start = pl.multiple_of(core * HALF, HALF)
    acc = jnp.zeros((HALF, F), F32)
    mass = jnp.zeros((HALF, 1), F32)
    for o in range(4):
        e, local, high, low = refs[4 * o : 4 * o + 4]
        stats = every[:, lax.rem(where[0] + o, 4)]
        maxes, sums = stats[:, 0], stats[:, 1]
        peak = jnp.max(maxes, axis=0, keepdims=True)
        total = jnp.sum(sums * jnp.exp(maxes - peak), axis=0, keepdims=True)
        w = e[pl.ds(start, HALF), :] * (jnp.exp(local[0:1] - peak) / total)
        mass = mass + jnp.sum(w, axis=1, keepdims=True)
        acc = acc + product(split(w), (high[...], low[...]), ((1,), (0,)))
    lane = lax.broadcasted_iota(jnp.int32, (8, LANES), 1) // 16
    for y in range(4):
        held = jnp.zeros((8, LANES), F32)
        for r in range(8):
            row = y * ROWS + r * 8
            for t in range(8):
                out[y, r * 8 + t] = acc[row : row + 8, t * LANES : (t + 1) * LANES]
            held = jnp.where(lane == r, mass[row : row + 8], held)
        out[y, ROWS] = held


def numerator(own, where, every, blocks):
    flat = [a for block in blocks for a in block]
    body = lambda *refs: numerator_body(own, *refs)
    out = shape(4, ROWS + 1, 8, LANES)
    return call(body, out, 1 + len(flat), 24 * HALF * BLOCK * F, smem=1)(where, every, *flat)


def gather_body(parts, out):
    out[...] = (parts[0] + parts[1]) + (parts[2] + parts[3])


def gather(parts):
    return call(gather_body, shape(ROWS + 1, 8, LANES), 1, 4 * ROWS * F)(parts)


def update_body(where, views, sums, out):
    start = pl.multiple_of(where[2], ROWS)
    mass = sums[0, ROWS] + sums[1, ROWS] + 1.0
    for r in range(8):
        scale = mass[:, 16 * r : 16 * r + 1]
        for t in range(8):
            k = r * 8 + t
            here = views[pl.ds(start + r * 8, 8), t * LANES : (t + 1) * LANES]
            new = (here + (sums[0, k] + sums[1, k])) / scale
            for y in range(4):
                out[y, k] = new


def update(*args):
    return call(update_body, shape(4, ROWS, 8, LANES), 2, 4 * ROWS * F, smem=1)(*args)


def em_round(images, views):
    core, y, x = lax.axis_index("c"), lax.axis_index("y"), lax.axis_index("x")
    n_views = views.shape[0]
    images, core, x, row, lower = lax.optimization_barrier((images, core, x, core * HALF + y * ROWS, core == 0))
    where = jnp.stack([x, core, row]).astype(jnp.int32)
    rows = images.reshape(-1, F)
    across = lax.ppermute(rows, "x", ACROSS)
    own = lax.all_gather(rows, "zl", axis=0, tiled=True)
    up = lax.ppermute(own, "x", UP)
    down = lax.ppermute(own, "x", DOWN)
    across, own = lax.optimization_barrier((across, own))
    far = lax.all_gather(across, "zl", axis=0, tiled=True)
    high = lax.reduce_precision(views, 8, 7)
    prepared = (high.astype(BF16), (views - high).astype(BF16))
    b_own, b_far = some(prepared, (own, far))
    b_down, b_up, every = rest(where, prepared, (down, up), (b_own[1], b_far[1]))
    every = lax.all_to_all(every, VIEW, 0, 0)
    blocks = (b_own, b_down, b_far, b_up)
    theirs = lax.ppermute(numerator(False, where, every, blocks), "c", SWAP)
    mine = numerator(True, where, every, blocks) + theirs
    sums = gather(lax.all_to_all(mine, "y", 0, 0))
    pair = lax.all_gather(sums, ("zh", "c"), axis=0, axis_index_groups=CROSS)
    sums = lax.all_gather(pair[0] + pair[1], ("zh", "c"), axis=0, axis_index_groups=UNCROSS)
    new = update(where, views, sums)
    new = lax.all_to_all(new, "y", 0, 0)
    other = lax.ppermute(new, "c", SWAP)
    both = jnp.where(lower, jnp.stack([new, other]), jnp.stack([other, new]))
    return both.reshape(n_views // 8, 8, 8, LANES).transpose(0, 2, 1, 3).reshape(n_views, F)


def solution(mesh):
    inner = Mesh(mesh.devices.reshape(4, 4, 2, 4, 4), AXES)
    placed = (P(None, AXES, None), P(VIEW, None))
    return jax.shard_map(em_round, mesh=inner, in_specs=placed, out_specs=P(VIEW, None), check_vma=False)
```

```python
import math

import jax
import jax.numpy as jnp
from jax import lax
from jax.experimental import pallas as pl
from jax.experimental.pallas import tpu as pltpu
from jax.sharding import Mesh, PartitionSpec as P

F = 1024
LANES = 128
BLOCK = 192
HALF = 256
ROWS = 64
AXES = ("y", "zh", "c", "x", "zl")
VIEW = ("x", "zl")
BETA = 1.6 / math.sqrt(F)
SWAP = [(0, 1), (1, 0)]
UP = [(i, (i + 1) % 4) for i in range(4)]
DOWN = [(i, (i - 1) % 4) for i in range(4)]
ACROSS = [(i, (i + 2) % 4) for i in range(4)]
EVEN, ODD = [(0, 1), (2, 3)], [(1, 2), (3, 0)]
CROSS = [[2 * a, 2 * b] for a, b in EVEN] + [[2 * a + 1, 2 * b + 1] for a, b in ODD]
UNCROSS = [[2 * a, 2 * b] for a, b in ODD] + [[2 * a + 1, 2 * b + 1] for a, b in EVEN]
VMEM = pl.BlockSpec(memory_space=pltpu.VMEM)
SMEM = pl.BlockSpec(memory_space=pltpu.SMEM)
BF16, F32 = jnp.bfloat16, jnp.float32


def shape(*dims, dtype=F32):
    return jax.ShapeDtypeStruct(dims, dtype)


def split(x):
    high = x.astype(BF16)
    return high, (x - high.astype(F32)).astype(BF16)


def product(a, b, dims):
    def dot(p, q):
        return lax.dot_general(p, q, (dims, ((), ())), preferred_element_type=F32)

    return dot(a[0], b[0]) + (dot(a[0], b[1]) + dot(a[1], b[0]))


def call(body, out, n_in, flops, smem=0):
    return pl.pallas_call(
        body,
        out_shape=out,
        in_specs=[SMEM] * smem + [VMEM] * n_in,
        out_specs=jax.tree.map(lambda _: VMEM, out),
        cost_estimate=pl.CostEstimate(flops=flops, bytes_accessed=4 << 20, transcendentals=0),
        compiler_params=pltpu.CompilerParams(vmem_limit_bytes=16 << 20),
    )


def prepare_body(views, high, low, norm):
    v = views[...]
    high[...], low[...] = split(v)
    norm[...] = jnp.broadcast_to(0.5 * jnp.sum(v * v, axis=1, keepdims=True), norm.shape)


def score(views, images, e, stats, high, low):
    pair = split(images[...])
    high[...], low[...] = pair
    dots = product((views[0][...], views[1][...]), pair, ((1,), (1,)))
    s = BETA * (dots - views[2][:, :1])
    peak = jnp.max(s, axis=0, keepdims=True)
    expo = jnp.exp(s - peak)
    e[...] = expo
    stats[...] = jnp.concatenate([peak, jnp.sum(expo, axis=0, keepdims=True)], axis=0)


def block_out(v):
    return [shape(v, BLOCK), shape(2, BLOCK), shape(BLOCK, F, dtype=BF16), shape(BLOCK, F, dtype=BF16)]


def some_body(*refs):
    views, n = refs[:3], (len(refs) - 3) // 5
    blocks, outs = refs[3 : 3 + n], refs[3 + n :]
    for k in range(n):
        score(views, blocks[k], *outs[4 * k : 4 * k + 4])


def some(prepared, blocks):
    v, n = prepared[0].shape[0], len(blocks)
    got = call(some_body, block_out(v) * n, 3 + n, 6 * n * BLOCK * v * F)(*prepared, *blocks)
    return [got[k : k + 4] for k in range(0, len(got), 4)]


def rest_body(where, *refs):
    views, blocks, known, outs, every = refs[:3], refs[3:5], refs[5:7], refs[7:15], refs[15]
    for k in range(2):
        score(views, blocks[k], *outs[4 * k : 4 * k + 4])
    for o, s in enumerate((known[0], outs[1], known[1], outs[5])):
        line = lax.rem(where[0] + o, 4)
        for k in range(16):
            every[k, line] = s[...]


def rest(where, prepared, blocks, stats):
    v = prepared[0].shape[0]
    out = block_out(v) * 2 + [shape(16, 4, 2, BLOCK)]
    got = call(rest_body, out, 7, 12 * BLOCK * v * F, smem=1)(where, *prepared, *blocks, *stats)
    return got[:4], got[4:8], got[8]


def numerator_body(own, where, *refs):
    if own:
        factors, blocks, out = refs[0], refs[1:-1], refs[-1]
    else:
        every, blocks, out, factors = refs[0], refs[1:-2], refs[-2], refs[-1]
    core = where[1] if own else 1 - where[1]
    start = pl.multiple_of(core * HALF, HALF)
    acc = jnp.zeros((HALF, F), F32)
    mass = jnp.zeros((HALF, 1), F32)
    for o in range(4):
        e, local, high, low = blocks[4 * o : 4 * o + 4]
        if own:
            factor = factors[o : o + 1]
        else:
            stats = every[:, lax.rem(where[0] + o, 4)]
            maxes, sums = stats[:, 0], stats[:, 1]
            peak = jnp.max(maxes, axis=0, keepdims=True)
            total = jnp.sum(sums * jnp.exp(maxes - peak), axis=0, keepdims=True)
            factor = jnp.exp(local[0:1] - peak) / total
            factors[o : o + 1] = factor
        w = e[pl.ds(start, HALF), :] * factor
        mass = mass + jnp.sum(w, axis=1, keepdims=True)
        acc = acc + product(split(w), (high[...], low[...]), ((1,), (0,)))
    lane = lax.broadcasted_iota(jnp.int32, (8, LANES), 1) // 16
    for y in range(4):
        held = jnp.zeros((8, LANES), F32)
        for r in range(8):
            row = y * ROWS + r * 8
            for t in range(8):
                out[y, r * 8 + t] = acc[row : row + 8, t * LANES : (t + 1) * LANES]
            held = jnp.where(lane == r, mass[row : row + 8], held)
        out[y, ROWS] = held


def numerator(own, where, lead, blocks):
    flat = [a for block in blocks for a in block]
    body = lambda *refs: numerator_body(own, *refs)
    out = [shape(4, ROWS + 1, 8, LANES)] + ([] if own else [shape(4, BLOCK)])
    got = call(body, out, 1 + len(flat), 24 * HALF * BLOCK * F, smem=1)(where, lead, *flat)
    return got[0] if own else got


def both_body(pair, out):
    out[...] = pair[0] + pair[1]


def both_of(pair):
    return call(both_body, shape(*pair.shape[1:]), 1, ROWS * F)(pair)


def gather_body(parts, out):
    out[...] = (parts[0] + parts[1]) + (parts[2] + parts[3])


def gather(parts):
    return call(gather_body, shape(ROWS + 1, 8, LANES), 1, 4 * ROWS * F)(parts)


def update_body(where, views, sums, out):
    start = pl.multiple_of(where[2], ROWS)
    mass = sums[0, ROWS] + sums[1, ROWS] + 1.0
    for r in range(8):
        scale = mass[:, 16 * r : 16 * r + 1]
        for t in range(8):
            k = r * 8 + t
            here = views[pl.ds(start + r * 8, 8), t * LANES : (t + 1) * LANES]
            new = (here + (sums[0, k] + sums[1, k])) / scale
            for y in range(4):
                out[y, k] = new


def update(*args):
    return call(update_body, shape(4, ROWS, 8, LANES), 2, 4 * ROWS * F, smem=1)(*args)


def em_round(images, views):
    core, y, x = lax.axis_index("c"), lax.axis_index("y"), lax.axis_index("x")
    n_views = views.shape[0]
    images, core, x, row, lower = lax.optimization_barrier((images, core, x, core * HALF + y * ROWS, core == 0))
    where = jnp.stack([x, core, row]).astype(jnp.int32)
    rows = images.reshape(-1, F)
    across = lax.ppermute(rows, "x", ACROSS)
    own = lax.all_gather(rows, "zl", axis=0, tiled=True)
    up = lax.ppermute(own, "x", UP)
    down = lax.ppermute(own, "x", DOWN)
    across, own = lax.optimization_barrier((across, own))
    far = lax.all_gather(across, "zl", axis=0, tiled=True)
    prepared = call(
        prepare_body,
        [shape(n_views, F, dtype=BF16), shape(n_views, F, dtype=BF16), shape(n_views, LANES)],
        1, 4 * n_views * F,
    )(views)
    b_own, b_far = some(prepared, (own, far))
    b_down, b_up, every = rest(where, prepared, (down, up), (b_own[1], b_far[1]))
    every = lax.all_to_all(every, VIEW, 0, 0)
    blocks = (b_own, b_down, b_far, b_up)
    theirs, factors = numerator(False, where, every, blocks)
    theirs = lax.ppermute(theirs, "c", SWAP)
    mine = numerator(True, where, factors, blocks) + theirs
    sums = gather(lax.all_to_all(mine, "y", 0, 0))
    pair = lax.all_gather(sums, ("zh", "c"), axis=0, axis_index_groups=CROSS)
    sums = lax.all_gather(both_of(pair), ("zh", "c"), axis=0, axis_index_groups=UNCROSS)
    new = update(where, views, sums)
    new = lax.all_to_all(new, "y", 0, 0)
    other = lax.ppermute(new, "c", SWAP)
    both = jnp.where(lower, jnp.stack([new, other]), jnp.stack([other, new]))
    return both.reshape(n_views // 8, 8, 8, LANES).transpose(0, 2, 1, 3).reshape(n_views, F)


def solution(mesh):
    inner = Mesh(mesh.devices.reshape(4, 4, 2, 4, 4), AXES)
    placed = (P(None, AXES, None), P(VIEW, None))
    return jax.shard_map(em_round, mesh=inner, in_specs=placed, out_specs=P(VIEW, None), check_vma=False)
```

```python
import math

import jax
import jax.numpy as jnp
from jax import lax
from jax.experimental import pallas as pl
from jax.experimental.pallas import tpu as pltpu
from jax.sharding import Mesh, PartitionSpec as P

F = 1024
LANES = 128
BLOCK = 192
HALF = 256
ROWS = 64
AXES = ("y", "zh", "c", "x", "zl")
VIEW = ("x", "zl")
BETA = 1.6 / math.sqrt(F)
SWAP = [(0, 1), (1, 0)]
UP = [(i, (i + 1) % 4) for i in range(4)]
DOWN = [(i, (i - 1) % 4) for i in range(4)]
ACROSS = [(i, (i + 2) % 4) for i in range(4)]
EVEN, ODD = [(0, 1), (2, 3)], [(1, 2), (3, 0)]
CROSS = [[2 * a, 2 * b] for a, b in EVEN] + [[2 * a + 1, 2 * b + 1] for a, b in ODD]
UNCROSS = [[2 * a, 2 * b] for a, b in ODD] + [[2 * a + 1, 2 * b + 1] for a, b in EVEN]
VMEM = pl.BlockSpec(memory_space=pltpu.VMEM)
SMEM = pl.BlockSpec(memory_space=pltpu.SMEM)
BF16, F32 = jnp.bfloat16, jnp.float32


def shape(*dims, dtype=F32):
    return jax.ShapeDtypeStruct(dims, dtype)


def split(x):
    high = x.astype(BF16)
    return high, (x - high.astype(F32)).astype(BF16)


def product(a, b, dims):
    def dot(p, q):
        return lax.dot_general(p, q, (dims, ((), ())), preferred_element_type=F32)

    return dot(a[0], b[0]) + (dot(a[0], b[1]) + dot(a[1], b[0]))


def call(body, out, n_in, flops, smem=0):
    return pl.pallas_call(
        body,
        out_shape=out,
        in_specs=[SMEM] * smem + [VMEM] * n_in,
        out_specs=jax.tree.map(lambda _: VMEM, out),
        cost_estimate=pl.CostEstimate(flops=flops, bytes_accessed=4 << 20, transcendentals=0),
        compiler_params=pltpu.CompilerParams(vmem_limit_bytes=16 << 20),
    )


def prepare_body(views, high, low, norm):
    v = views[...]
    high[...], low[...] = split(v)
    norm[...] = jnp.broadcast_to(0.5 * jnp.sum(v * v, axis=1, keepdims=True), norm.shape)


def score(views, images, e, stats, high, low):
    pair = split(images[...])
    high[...], low[...] = pair
    dots = product((views[0][...], views[1][...]), pair, ((1,), (1,)))
    s = BETA * (dots - views[2][:, :1])
    peak = jnp.max(s, axis=0, keepdims=True)
    expo = jnp.exp(s - peak)
    e[...] = expo
    stats[...] = jnp.concatenate([peak, jnp.sum(expo, axis=0, keepdims=True)], axis=0)


def block_out(v):
    return [shape(v, BLOCK), shape(2, BLOCK), shape(BLOCK, F, dtype=BF16), shape(BLOCK, F, dtype=BF16)]


def some_body(*refs):
    views, n = refs[:3], (len(refs) - 3) // 5
    blocks, outs = refs[3 : 3 + n], refs[3 + n :]
    for k in range(n):
        score(views, blocks[k], *outs[4 * k : 4 * k + 4])


def some(prepared, blocks):
    v, n = prepared[0].shape[0], len(blocks)
    got = call(some_body, block_out(v) * n, 3 + n, 6 * n * BLOCK * v * F)(*prepared, *blocks)
    return [got[k : k + 4] for k in range(0, len(got), 4)]


def rest_body(where, *refs):
    views, blocks, known, outs, every = refs[:3], refs[3:5], refs[5:7], refs[7:15], refs[15]
    for k in range(2):
        score(views, blocks[k], *outs[4 * k : 4 * k + 4])
    for o, s in enumerate((known[0], outs[1], known[1], outs[5])):
        line = lax.rem(where[0] + o, 4)
        for k in range(16):
            every[k, line] = s[...]


def rest(where, prepared, blocks, stats):
    v = prepared[0].shape[0]
    out = block_out(v) * 2 + [shape(16, 4, 2, BLOCK)]
    got = call(rest_body, out, 7, 12 * BLOCK * v * F, smem=1)(where, *prepared, *blocks, *stats)
    return got[:4], got[4:8], got[8]


def numerator_body(own, where, *refs):
    if own:
        factors, blocks, out = refs[0], refs[1:-1], refs[-1]
    else:
        every, blocks, out, factors = refs[0], refs[1:-2], refs[-2], refs[-1]
    core = where[1] if own else 1 - where[1]
    start = pl.multiple_of(core * HALF, HALF)
    acc = jnp.zeros((HALF, F), F32)
    mass = jnp.zeros((HALF, 1), F32)
    for o in range(4):
        e, local, high, low = blocks[4 * o : 4 * o + 4]
        if own:
            factor = factors[o : o + 1]
        else:
            stats = every[:, lax.rem(where[0] + o, 4)]
            maxes, sums = stats[:, 0], stats[:, 1]
            peak = jnp.max(maxes, axis=0, keepdims=True)
            total = jnp.sum(sums * jnp.exp(maxes - peak), axis=0, keepdims=True)
            factor = jnp.exp(local[0:1] - peak) / total
            factors[o : o + 1] = factor
        w = e[pl.ds(start, HALF), :] * factor
        mass = mass + jnp.sum(w, axis=1, keepdims=True)
        acc = acc + product(split(w), (high[...], low[...]), ((1,), (0,)))
    lane = lax.broadcasted_iota(jnp.int32, (8, LANES), 1) // 16
    for y in range(4):
        held = jnp.zeros((8, LANES), F32)
        for r in range(8):
            row = y * ROWS + r * 8
            for t in range(8):
                out[y, r * 8 + t] = acc[row : row + 8, t * LANES : (t + 1) * LANES]
            held = jnp.where(lane == r, mass[row : row + 8], held)
        out[y, ROWS] = held


def numerator(own, where, lead, blocks):
    flat = [a for block in blocks for a in block]
    body = lambda *refs: numerator_body(own, *refs)
    out = [shape(4, ROWS + 1, 8, LANES)] + ([] if own else [shape(4, BLOCK)])
    got = call(body, out, 1 + len(flat), 24 * HALF * BLOCK * F, smem=1)(where, lead, *flat)
    return got[0] if own else got


def both_body(pair, out):
    out[...] = pair[0] + pair[1]


def both_of(pair):
    return call(both_body, shape(*pair.shape[1:]), 1, ROWS * F)(pair)


def gather_body(parts, out):
    out[...] = (parts[0] + parts[1]) + (parts[2] + parts[3])


def gather(parts):
    return call(gather_body, shape(ROWS + 1, 8, LANES), 1, 4 * ROWS * F)(parts)


def update_body(where, views, sums, out):
    start = pl.multiple_of(where[2], ROWS)
    inverse = 1.0 / (sums[0, ROWS] + sums[1, ROWS] + 1.0)
    for r in range(8):
        scale = inverse[:, 16 * r : 16 * r + 1]
        for t in range(8):
            k = r * 8 + t
            here = views[pl.ds(start + r * 8, 8), t * LANES : (t + 1) * LANES]
            new = (here + (sums[0, k] + sums[1, k])) * scale
            for y in range(4):
                out[y, k] = new


def update(*args):
    return call(update_body, shape(4, ROWS, 8, LANES), 2, 4 * ROWS * F, smem=1)(*args)


def em_round(images, views):
    core, y, x = lax.axis_index("c"), lax.axis_index("y"), lax.axis_index("x")
    n_views = views.shape[0]
    images, core, x, row, lower = lax.optimization_barrier((images, core, x, core * HALF + y * ROWS, core == 0))
    where = jnp.stack([x, core, row]).astype(jnp.int32)
    rows = images.reshape(-1, F)
    across = lax.ppermute(rows, "x", ACROSS)
    own = lax.all_gather(rows, "zl", axis=0, tiled=True)
    up = lax.ppermute(own, "x", UP)
    down = lax.ppermute(own, "x", DOWN)
    across, own = lax.optimization_barrier((across, own))
    far = lax.all_gather(across, "zl", axis=0, tiled=True)
    prepared = call(
        prepare_body,
        [shape(n_views, F, dtype=BF16), shape(n_views, F, dtype=BF16), shape(n_views, LANES)],
        1, 4 * n_views * F,
    )(views)
    b_own, b_far = some(prepared, (own, far))
    b_down, b_up, every = rest(where, prepared, (down, up), (b_own[1], b_far[1]))
    every = lax.all_to_all(every, VIEW, 0, 0)
    blocks = (b_own, b_down, b_far, b_up)
    theirs, factors = numerator(False, where, every, blocks)
    theirs = lax.ppermute(theirs, "c", SWAP)
    mine = numerator(True, where, factors, blocks) + theirs
    sums = gather(lax.all_to_all(mine, "y", 0, 0))
    pair = lax.all_gather(sums, ("zh", "c"), axis=0, axis_index_groups=CROSS)
    sums = lax.all_gather(both_of(pair), ("zh", "c"), axis=0, axis_index_groups=UNCROSS)
    new = update(where, views, sums)
    new = lax.all_to_all(new, "y", 0, 0)
    other = lax.ppermute(new, "c", SWAP)
    both = jnp.where(lower, jnp.stack([new, other]), jnp.stack([other, new]))
    return both.reshape(n_views // 8, 8, 8, LANES).transpose(0, 2, 1, 3).reshape(n_views, F)


def solution(mesh):
    inner = Mesh(mesh.devices.reshape(4, 4, 2, 4, 4), AXES)
    placed = (P(None, AXES, None), P(VIEW, None))
    return jax.shard_map(em_round, mesh=inner, in_specs=placed, out_specs=P(VIEW, None), check_vma=False)
```
